32 devices in a mesh: member: 8 (over y, x, core), band: 4 (over z).
Axes of the slice: x: 2, y: 2, z: 4, core: 2. Of those that a mesh axis runs over, the one named last changes fastest.
Arguments:
- controls: float32 [16, 16, 256, 512], P('member', None, 'band'), may hold values from -6 to 6
- members: float32 [16, 16, 256, 512], P('member', None, 'band'), may hold values from -6 to 6
- loc_lon: float32 [512, 512], replicated, may hold values from -0.25 to 0.25
- loc_lat: float32 [256, 256], replicated, may hold values from -0.375 to 0.375
- balance: float32 [5, 1024, 2048], P(None, 'band', 'member'), may hold values from -1 to 1
- innovation: float32 [16, 1024, 2048], P(None, 'band', 'member'), may hold values from -6 to 6
- obs_weight: float32 [16, 1024, 2048], P(None, 'band', 'member'), may hold values from 0.2 to 5
Outputs:
- gradient: float32 [16, 16, 256, 512], P('member', None, 'band')
The draws below stay inside these ranges and needn't reach their ends.
All inputs are finite; a program needn't handle non-finite values.
Results may differ from the reference program's by a relative error of at most 0.00012.
Values sent between devices are 32-bit elements; how exact they have to be, the bound alone decides.
No kernel may reach another device: no remote copies, remote signals or barrier semaphores. Data moves between devices by JAX's collectives and lax.ppermute only.
A program may use at most 128 MiB of HBM per device.

```python
import math
import jax
import jax.numpy as jnp
from jax import lax

LEVELS = 16
NYC = 256
NXC = 512
KEN = 16
NYF = 1024
NXF = 2048


def level_of(rng, dims, shards, smallest, high):
    def one(axis_at, shards_of):
        steps = jax.random.uniform(jax.random.fold_in(jax.random.fold_in(rng, 6), axis_at), (shards_of,), jnp.float32, smallest / len(shards), high / len(shards))
        return jnp.repeat(jnp.exp(steps), dims[axis_at] // shards_of).reshape((-1,) + (1,) * (len(dims) - axis_at - 1))

    loudness = one(*shards[0])
    for cut in shards[1:]:
        loudness = loudness * one(*cut)
    return loudness


def normal_values(key, shape, deviation, bound, cuts=(), kind=jnp.bfloat16):
    drawn = deviation * jax.random.normal(key, shape, jnp.float32)
    if cuts:
        drawn = drawn * level_of(key, shape, cuts, -0.22, 0.18)
    return jnp.clip(drawn, -bound, bound).astype(kind)


def setup_inputs(seed: int = 0) -> dict:
    arg_keys = jax.random.split(jax.random.key(seed), 8)
    controls = normal_values(arg_keys[0], (KEN, LEVELS, NYC, NXC), 1.0, 6.0, ((0, 8), (2, 4)), jnp.float32)
    members = normal_values(arg_keys[1], (KEN, LEVELS, NYC, NXC), 1.0, 6.0, ((0, 8), (2, 4)), jnp.float32)
    loc_lon = normal_values(arg_keys[2], (NXC, NXC), NXC ** -0.5, 0.25, (), jnp.float32)
    loc_lat = normal_values(arg_keys[3], (NYC, NYC), NYC ** -0.5, 0.375, (), jnp.float32)
    balance = jnp.clip(jax.random.uniform(arg_keys[4], (5, NYF, NXF), jnp.float32, -1.0, 1.0) * level_of(arg_keys[4], (5, NYF, NXF), ((1, 4), (2, 8)), -0.4, 0.0), -1.0, 1.0)
    innovation = normal_values(arg_keys[5], (LEVELS, NYF, NXF), 1.0, 6.0, ((1, 4), (2, 8)), jnp.float32)
    obs_weight = jnp.clip(jnp.exp(math.log(5.0) - 3.218876 * jax.random.uniform(arg_keys[6], (LEVELS, NYF, NXF), jnp.float32) ** level_of(arg_keys[6], (LEVELS, NYF, NXF), ((1, 4), (2, 8)), -0.2, 0.2)), 0.2, 5.0)
    return {"controls": controls, "members": members, "loc_lon": loc_lon, "loc_lat": loc_lat, "balance": balance, "innovation": innovation, "obs_weight": obs_weight}


phase_fraction = (0.625, 0.875, 0.125, 0.375)
phase_start = (0, 0, 1, 1)

def cubic_weights(fraction):
    return ((-fraction ** 3 + 2 * fraction ** 2 - fraction) / 2, (3 * fraction ** 3 - 5 * fraction ** 2 + 2) / 2, (-3 * fraction ** 3 + 4 * fraction ** 2 + fraction) / 2, (fraction ** 3 - fraction ** 2) / 2)

def refine(padded, dim_index):
    length = padded.shape[dim_index] - 4
    phase_rows = []
    for phase_index in range(4):
        weights = cubic_weights(phase_fraction[phase_index])
        summed = jnp.zeros_like(lax.slice_in_dim(padded, 0, length, axis=dim_index))
        for tap_index in range(4):
            first = phase_start[phase_index] + tap_index
            summed = summed + weights[tap_index] * lax.slice_in_dim(padded, first, first + length, axis=dim_index)
        phase_rows.append(summed)
    stacked = jnp.stack(phase_rows, axis=dim_index + 1)
    new_shape = list(padded.shape)
    new_shape[dim_index] = 4 * length
    return stacked.reshape(new_shape)

def refine_both(padded):
    return refine(refine(padded, 1), 2)

def apply_balance(fine_field, balance):
    grown_field = jnp.pad(fine_field, ((0, 0), (1, 1), (0, 0)))
    grown_field = jnp.concatenate([grown_field[:, :, -1:], grown_field, grown_field[:, :, :1]], axis=2)
    return balance[0] * fine_field + balance[1] * grown_field[:, 1:-1, 2:] + balance[2] * grown_field[:, 1:-1, :-2] + balance[3] * grown_field[:, 2:, 1:-1] + balance[4] * grown_field[:, :-2, 1:-1]

def reference(controls, members, loc_lon, loc_lat, balance, innovation, obs_weight):
    highest = lax.Precision.HIGHEST
    member_scale = 1.0 / math.sqrt(controls.shape[0] - 1)
    rowwise = jnp.einsum('klyx,ux->klyu', controls, loc_lon, precision=highest)
    fields = jnp.einsum('vy,klyx->klvx', loc_lat, rowwise, precision=highest)
    increment = lax.optimization_barrier(jnp.sum(members * fields, axis=0)) * member_scale

    def obs_cost(coarse):
        padded = jnp.pad(coarse, ((0, 0), (2, 2), (0, 0)))
        padded = jnp.concatenate([padded[:, :, -2:], padded, padded[:, :, :2]], axis=2)
        image = apply_balance(refine_both(padded), balance)
        misfit = image - innovation
        return 0.5 * jnp.sum(obs_weight * misfit * misfit)
    coarse_grad = jax.grad(obs_cost)(increment)
    weighted = members * coarse_grad[None] * member_scale
    adjoint = jnp.einsum('klyu,ux->klyx', weighted, loc_lon, precision=highest)
    adjoint = jnp.einsum('vy,klvx->klyx', loc_lat, adjoint, precision=highest)
    return controls + adjoint
```

```python
import functools
import math

import jax
import jax.numpy as jnp
import numpy as np
from jax import lax
from jax.experimental import pallas as pl
from jax.experimental.pallas import tpu as pltpu
from jax.sharding import PartitionSpec as P


F32, BF16 = jnp.float32, jnp.bfloat16
phase_fraction = (0.625, 0.875, 0.125, 0.375)
phase_start = (0, 0, 1, 1)
NN = (((1,), (0,)), ((), ()))
NT = (((1,), (1,)), ((), ()))
TN = (((0,), (0,)), ((), ()))


def cubic_weights(fraction):
    return (
        (-(fraction**3) + 2 * fraction**2 - fraction) / 2,
        (3 * fraction**3 - 5 * fraction**2 + 2) / 2,
        (-3 * fraction**3 + 4 * fraction**2 + fraction) / 2,
        (fraction**3 - fraction**2) / 2,
    )


def round_up(value, step):
    return -(-value // step) * step


def edged_matrix(coarse, rows_out, cols_out):
    matrix = np.zeros((rows_out, cols_out), np.float32)
    fine = 4 * coarse
    for row, at in [(i, i) for i in range(fine + 1)] + [(-1, rows_out - 1)]:
        cell, phase = divmod(row, 4)
        for tap, weight in enumerate(cubic_weights(phase_fraction[phase])):
            matrix[at, cell + phase_start[phase] + tap] += weight
    return matrix


def split(value):
    high = value.astype(BF16)
    return high, (value - high.astype(F32)).astype(BF16)


def outer_split(value):
    high = lax.reduce_precision(value, 8, 7)
    return high.astype(BF16), lax.reduce_precision(value - high, 8, 7).astype(BF16)


def three(value, axis):
    high, low = split(value)
    return jnp.concatenate([high, low, high], axis=axis)


def outer_three(value, axis):
    high, low = outer_split(value)
    return jnp.concatenate([high, high, low], axis=axis)


def dot(left, right, dims):
    return lax.dot_general(left, right, dims, preferred_element_type=F32)


def field_kernel(scale, members, bands, *refs):
    pieces, lat, lon, out, wrapped = refs[:bands], *refs[bands:]
    full = lat.shape[1] // 3, lon.shape[0]
    stripe = pieces[0].shape[3]
    total = None
    for k in range(members):
        ctrl = jnp.concatenate([p[0, k, 0] for p in pieces], axis=0)
        rowwise = dot(three(ctrl, 1), lon[...], NT)
        field = dot(lat[...], three(rowwise, 0), NN)
        product = jnp.concatenate([p[1, k, 0] for p in pieces], axis=0) * field
        total = product if total is None else total + product
    nx = full[1]
    wrapped[8 : 8 + nx, :] = (total * scale).T
    wrapped[0:8, :] = wrapped[nx : nx + 8, :]
    wrapped[nx + 8 : nx + 16, :] = wrapped[8:16, :]
    windows, _, width, _ = out.shape
    step = nx // windows
    for m in range(windows):
        start = min(step * m + 6, nx + 16 - width)
        lag = step * m + 6 - start
        rows = wrapped[start : start + width, :]
        out[m, 0] = pltpu.roll(rows, width - lag, 0) if lag else rows


def window_kernel(stripe, parts, *outs):
    total = parts[0, 0]
    for m in range(1, parts.shape[0]):
        total = total + parts[m, 0]
    lats = total.shape[1]
    for s, out in enumerate(outs):
        turned = pltpu.roll(total, (2 - stripe * s) % lats, 1)
        out[0] = turned[:, : out.shape[2]]


def fine_kernel(bands, band_ref, *refs):
    wins, (inn, weight, balance, rl3, ru3, rl_hi, rl_lo, rub3) = refs[:bands], refs[bands : bands + 8]
    outs, window = refs[bands + 8 : -1], refs[-1]
    owner, level = pl.program_id(0), pl.program_id(1)
    for s in range(bands):

        @pl.when(owner == s)
        def _():
            window[...] = wins[s][level]

    nlat, nlon = inn.shape[1:]
    tall, wide = rl3.shape[0], ru3.shape[1]
    width = window.shape[0]
    win = three(window[...], 1)
    part = dot(rl3[...], jnp.concatenate([win] * 3, axis=0), NT)
    high = part.astype(BF16).astype(F32)
    lane = lax.broadcasted_iota(jnp.int32, part.shape, 1)
    part = jnp.where((lane >= width) & (lane < 2 * width), part - high, high).astype(BF16)
    field = dot(part, ru3[...], NN)
    centre = field[:, :nlon]
    image = (
        balance[0] * centre[:nlat]
        + balance[1] * pltpu.roll(field, wide - 1, 1)[:nlat, :nlon]
        + balance[2] * pltpu.roll(field, 1, 1)[:nlat, :nlon]
        + balance[3] * pltpu.roll(centre, tall - 1, 0)[:nlat]
        + balance[4] * pltpu.roll(centre, 1, 0)[:nlat]
    )
    misfit = weight[0] * (image - inn[0])

    def longer(value):
        return jnp.concatenate([value, jnp.zeros((value.shape[0], wide - nlon), F32)], axis=1)

    def taller(value):
        return jnp.concatenate([value, jnp.zeros((tall - nlat, value.shape[1]), F32)], axis=0)

    across = (
        longer(balance[0] * misfit)
        + pltpu.roll(longer(balance[1] * misfit), 1, 1)
        + pltpu.roll(longer(balance[2] * misfit), wide - 1, 1)
    )
    along = pltpu.roll(taller(balance[3] * misfit), 1, 0) + pltpu.roll(taller(balance[4] * misfit), tall - 1, 0)
    grad = taller(across) + longer(along)
    back = dot(three(grad, 1), rub3[...], NT).T
    high, low = split(back)
    result = dot(high, rl_hi[...], NN) + (dot(high, rl_lo[...], NN) + dot(low, rl_hi[...], NN))
    for s in range(bands):

        @pl.when(owner == s)
        def _():
            outs[s][level] = result


def overlap_kernel(stripe, *refs):
    parts, out = refs[:-1], refs[-1]
    width, lats = out.shape[2:]
    total = None
    for s, part in enumerate(parts):
        window = part[0]
        grown = jnp.concatenate([window, jnp.zeros((width, lats - window.shape[1]), F32)], axis=1)
        turned = pltpu.roll(grown, (stripe * s - 2) % lats, 1)
        total = turned if total is None else total + turned
    for m in range(out.shape[0]):
        out[m, 0] = total


def adjoint_kernel(scale, members, bands, grads, *refs):
    pieces, lat, lon, wrapped = refs[:bands], refs[bands], refs[bands + 1], refs[-1]
    outs = refs[bands + 2 : 2 * bands + 2]
    stripe = pieces[0].shape[3]
    nx = lon.shape[1]
    wrapped[...] = jnp.zeros_like(wrapped)
    windows, _, width, _ = grads.shape
    step = nx // windows
    for m in range(windows):
        start = min(step * m + 6, nx + 16 - width)
        lag = step * m + 6 - start
        rows = pltpu.roll(grads[m, 0], lag, 0) if lag else grads[m, 0]
        wrapped[start : start + width, :] = wrapped[start : start + width, :] + rows
    wrapped[nx : nx + 8, :] = wrapped[nx : nx + 8, :] + wrapped[0:8, :]
    wrapped[8:16, :] = wrapped[8:16, :] + wrapped[nx + 8 : nx + 16, :]
    grad = wrapped[8 : 8 + nx, :].T * scale
    for k in range(members):
        weighted = jnp.concatenate([p[0, k, 0] for p in pieces], axis=0) * grad
        half = dot(lat[...], three(weighted, 0), NN)
        result = dot(three(half, 1), lon[...], NN)
        for s in range(bands):
            outs[s][k, 0] = result[stripe * s : stripe * (s + 1), :]


def add_kernel(bands, band_ref, ctrl, *refs):
    pieces, out = refs[:bands], refs[-1]
    band = band_ref[0]
    for s in range(bands):
        owner = lax.rem(band - s + bands, bands)
        out[0, owner, 0] = ctrl[0, owner, 0] + pieces[s][0, 0]


def scalar_grid(grid, in_specs, out_specs, scratch=()):
    return pltpu.PrefetchScalarGridSpec(
        num_scalar_prefetch=1, grid=grid, in_specs=in_specs, out_specs=out_specs, scratch_shapes=scratch
    )


def whole_block(array):
    return pl.BlockSpec(array.shape, lambda *ids: (0,) * len(array.shape))


def chunks_of(owned):
    if owned < 4:
        return [(c, 1) for c in range(owned)]
    head = owned // 2
    rest = owned - head
    return [(0, head)] + [(head + c, 1) for c in range(rest)]


def body(controls, members, loc_lon, loc_lat, balance, innovation, obs_weight):
    bands, mates = lax.axis_size("band"), lax.axis_size("member")
    band = lax.axis_index("band")
    band_array = jnp.reshape(band, (1,)).astype(jnp.int32)
    held, levels, cy, nx = controls.shape
    ny = loc_lat.shape[0]
    cx = nx // mates
    owned = levels // bands
    width = round_up(cx + 4, 16)
    lanes = min(round_up(cy + 4, 128), ny)
    nlat, nlon = innovation.shape[1:]
    tall, wide = nlat + 8, round_up(nlon + 2, 128)
    scale = 1.0 / math.sqrt(held * mates - 1)

    turned = jnp.roll(loc_lat, (-cy * band, -cy * band), (0, 1))
    lat3, lat_t3 = outer_three(turned, 1), outer_three(turned.T, 1)
    lon3, lon_b3 = outer_three(loc_lon, 1), outer_three(loc_lon, 0)
    ru = jnp.asarray(edged_matrix(cx, wide, width).T)
    ru3, rub3 = outer_three(ru, 0), outer_three(ru, 1)
    row = lax.broadcasted_iota(jnp.int32, (tall, lanes), 0)
    col = lax.broadcasted_iota(jnp.int32, (tall, lanes), 1)
    first, last = band == 0, band == bands - 1
    off = (first & ((row == tall - 1) | (col < 2))) | (last & ((row == nlat) | (col >= cy + 2)))
    rl = jnp.where(off, 0.0, jnp.asarray(edged_matrix(cy, tall, lanes)))
    rl3, (rl_hi, rl_lo) = outer_three(rl, 1), outer_split(rl)

    ctrl_view = controls.reshape(held, bands, owned, cy, nx)
    mem_view = members.reshape(held, bands, owned, cy, nx)
    wrap_scratch = pltpu.VMEM((nx + 16, ny), F32)

    def shifted(value, s):
        if s % bands == 0:
            return value
        return lax.ppermute(value, "band", [(i, (i + s) % bands) for i in range(bands)])

    def sent(first_level, count, s):
        at = lax.rem(band - s + bands, bands)
        size = (held, 1, count, cy, nx)
        start = (0, at, first_level, 0, 0)
        pair = [lax.dynamic_slice(v, start, size)[:, 0] for v in (ctrl_view, mem_view)]
        return jnp.stack(pair)

    def forward_parts(pieces, count):
        block = pl.BlockSpec((2, held, 1, cy, nx), lambda l: (0, 0, l, 0, 0))
        consts = (lat3, lon3)
        return pl.pallas_call(
            functools.partial(field_kernel, scale, held, bands),
            grid=(count,),
            in_specs=[block] * bands + [whole_block(c) for c in consts],
            out_specs=pl.BlockSpec((mates, 1, width, ny), lambda l: (0, l, 0, 0)),
            scratch_shapes=[wrap_scratch],
            out_shape=jax.ShapeDtypeStruct((mates, count, width, ny), F32),
            name="fields",
        )(*pieces, *consts)

    def windows(parts, count):
        return pl.pallas_call(
            functools.partial(window_kernel, cy),
            grid=(count,),
            in_specs=[pl.BlockSpec((mates, 1, width, ny), lambda l: (0, l, 0, 0))],
            out_specs=[pl.BlockSpec((1, width, lanes), lambda l: (l, 0, 0))] * bands,
            out_shape=[jax.ShapeDtypeStruct((count, width, lanes), F32)] * bands,
            name="windows",
        )(parts)

    def fine(wins, first_level, count):
        def level(o, l, b):
            return (lax.rem(b[0] - o + bands, bands) * owned + first_level + l, 0, 0)

        consts = (balance, rl3, ru3, rl_hi, rl_lo, rub3)
        shape = jax.ShapeDtypeStruct((count, width, lanes), F32)
        return pl.pallas_call(
            functools.partial(fine_kernel, bands),
            grid_spec=scalar_grid(
                (bands, count),
                [whole_block(w) for w in wins]
                + [pl.BlockSpec((1, nlat, nlon), level)] * 2
                + [whole_block(c) for c in consts],
                [whole_block(shape)] * bands,
                [pltpu.VMEM((width, lanes), F32)],
            ),
            out_shape=[shape] * bands,
            name="fine",
        )(band_array, *wins, innovation, obs_weight, *consts)

    def overlapped(parts, count):
        return pl.pallas_call(
            functools.partial(overlap_kernel, cy),
            grid=(count,),
            in_specs=[pl.BlockSpec((1, width, lanes), lambda l: (l, 0, 0))] * bands,
            out_specs=pl.BlockSpec((mates, 1, width, ny), lambda l: (0, l, 0, 0)),
            out_shape=jax.ShapeDtypeStruct((mates, count, width, ny), F32),
            name="overlapped",
        )(*parts)

    def backward_parts(grads, pieces, count):
        block = pl.BlockSpec((1, held, 1, cy, nx), lambda l: (1, 0, l, 0, 0))
        consts = (lat_t3, lon_b3)
        return pl.pallas_call(
            functools.partial(adjoint_kernel, scale, held, bands),
            grid=(count,),
            in_specs=[pl.BlockSpec((mates, 1, width, ny), lambda l: (0, l, 0, 0))]
            + [block] * bands
            + [whole_block(c) for c in consts],
            out_specs=[pl.BlockSpec((held, 1, cy, nx), lambda l: (0, l, 0, 0))] * bands,
            scratch_shapes=[wrap_scratch],
            out_shape=[jax.ShapeDtypeStruct((held, count, cy, nx), F32)] * bands,
            name="adjoint",
        )(grads, *pieces, *consts)

    def added(result, pieces, first_level, count):
        block = pl.BlockSpec((1, bands, 1, cy, nx), lambda k, l, b: (k, 0, first_level + l, 0, 0))
        piece = pl.BlockSpec((1, 1, cy, nx), lambda k, l, b: (k, l, 0, 0))
        carried = [] if result is None else [result]
        return pl.pallas_call(
            functools.partial(add_kernel, bands),
            grid_spec=scalar_grid(
                (held, count),
                [block] + [piece] * bands + [pl.BlockSpec(memory_space=pl.ANY)] * len(carried),
                block,
            ),
            out_shape=jax.ShapeDtypeStruct(ctrl_view.shape, F32),
            input_output_aliases={2 + bands: 0} if carried else {},
            name="added",
        )(band_array, ctrl_view, *pieces, *carried)

    plan = chunks_of(owned)
    received = [[shifted(sent(f, n, s), -s) for s in range(bands)] for f, n in plan]
    swap = functools.partial(lax.all_to_all, split_axis=0, concat_axis=0, tiled=True)
    result = None
    for (f, n), pieces in zip(plan, received):
        parts = swap(forward_parts(pieces, n), "member")
        wins = [shifted(w, s) for s, w in enumerate(windows(parts, n))]
        coarse = [shifted(g, -s) for s, g in enumerate(fine(wins, f, n))]
        grads = swap(overlapped(coarse, n), "member")
        back = backward_parts(grads, pieces, n)
        back = [shifted(p, s) for s, p in enumerate(back)]
        result = added(result, back, f, n)
    return result.reshape(controls.shape)


def solution(mesh):
    return jax.shard_map(
        body,
        mesh=mesh,
        in_specs=(
            P("member", None, "band", None),
            P("member", None, "band", None),
            P(),
            P(),
            P(None, "band", "member"),
            P(None, "band", "member"),
            P(None, "band", "member"),
        ),
        out_specs=P("member", None, "band", None),
        check_vma=False,
    )
```

```python
import functools
import math

import jax
import jax.numpy as jnp
import numpy as np
from jax import lax
from jax.experimental import pallas as pl
from jax.experimental.pallas import tpu as pltpu
from jax.sharding import PartitionSpec as P


F32, BF16 = jnp.float32, jnp.bfloat16
phase_fraction = (0.625, 0.875, 0.125, 0.375)
phase_start = (0, 0, 1, 1)
NN = (((1,), (0,)), ((), ()))
NT = (((1,), (1,)), ((), ()))


def cubic_weights(fraction):
    return (
        (-(fraction**3) + 2 * fraction**2 - fraction) / 2,
        (3 * fraction**3 - 5 * fraction**2 + 2) / 2,
        (-3 * fraction**3 + 4 * fraction**2 + fraction) / 2,
        (fraction**3 - fraction**2) / 2,
    )


def round_up(value, step):
    return -(-value // step) * step


def edged_matrix(coarse, rows_out, cols_out):
    matrix = np.zeros((rows_out, cols_out), np.float32)
    fine = 4 * coarse
    for row, at in [(i, i) for i in range(fine + 1)] + [(-1, rows_out - 1)]:
        cell, phase = divmod(row, 4)
        for tap, weight in enumerate(cubic_weights(phase_fraction[phase])):
            matrix[at, cell + phase_start[phase] + tap] += weight
    return matrix


def split(value):
    high = value.astype(BF16)
    return high, (value - high.astype(F32)).astype(BF16)


def outer_split(value):
    high = lax.reduce_precision(value, 8, 7)
    return high.astype(BF16), lax.reduce_precision(value - high, 8, 7).astype(BF16)


def three(value, axis):
    high, low = split(value)
    return jnp.concatenate([high, low, high], axis=axis)


def outer_three(value, axis):
    high, low = outer_split(value)
    return jnp.concatenate([high, high, low], axis=axis)


def dot(left, right, dims):
    return lax.dot_general(left, right, dims, preferred_element_type=F32)


def fields_of(scale, ctrls, perts, lat, lon, wrapped, out):
    nx = lon.shape[0]
    total = None
    for k in range(ctrls[0].shape[0]):
        ctrl = jnp.concatenate([p[k] for p in ctrls], axis=0)
        rowwise = dot(three(ctrl, 1), lon[...], NT)
        field = dot(lat[...], three(rowwise, 0), NN)
        product = jnp.concatenate([p[k] for p in perts], axis=0) * field
        total = product if total is None else total + product
    wrapped[8 : 8 + nx, :] = (total * scale).T
    wrapped[0:8, :] = wrapped[nx : nx + 8, :]
    wrapped[nx + 8 : nx + 16, :] = wrapped[8:16, :]
    windows, _, width, _ = out.shape
    step = nx // windows
    for m in range(windows):
        out[m, 0] = wrapped[step * m + 6 : step * m + 6 + width, :]


def overlapped(stripe, parts, out):
    windows, _, width, lats = out.shape
    total = None
    for s, part in enumerate(parts):
        window = part[...]
        grown = jnp.concatenate([window, jnp.zeros((width, lats - window.shape[1]), F32)], axis=1)
        turned = pltpu.roll(grown, (stripe * s - 2) % lats, 1)
        total = turned if total is None else total + turned
    for m in range(windows):
        out[m, out.shape[1] - 1] = total


def windows_of(stripe, parts, outs):
    total = parts[0, 0]
    for m in range(1, parts.shape[0]):
        total = total + parts[m, 0]
    lats = total.shape[1]
    for s, out in enumerate(outs):
        turned = pltpu.roll(total, (2 - stripe * s) % lats, 1)
        out[0] = turned[:, : out.shape[2]]


def adjoint_of(scale, grads, perts, lat, lon, wrapped, outs):
    stripe = perts[0].shape[1]
    nx = lon.shape[1]
    wrapped[...] = jnp.zeros_like(wrapped)
    windows, parts, width, _ = grads.shape
    step = nx // windows
    for m in range(windows):
        place = slice(step * m + 6, step * m + 6 + width)
        wrapped[place, :] = wrapped[place, :] + grads[m, parts - 1]
    wrapped[nx : nx + 8, :] = wrapped[nx : nx + 8, :] + wrapped[0:8, :]
    wrapped[8:16, :] = wrapped[8:16, :] + wrapped[nx + 8 : nx + 16, :]
    grad = wrapped[8 : 8 + nx, :].T * scale
    for k in range(perts[0].shape[0]):
        weighted = jnp.concatenate([p[k] for p in perts], axis=0) * grad
        half = dot(lat[...], three(weighted, 0), NN)
        result = dot(three(half, 1), lon[...], NN)
        for s, out in enumerate(outs):
            out[k] = result[stripe * s : stripe * (s + 1), :]


def fine_level(window, inn, weight, balance, rl3, ru3, rl_hi, rl_lo, rub3):
    nlat, nlon = inn.shape
    tall, wide = rl3.shape[0], ru3.shape[1]
    width = window.shape[0]
    win = three(window, 1)
    part = dot(rl3[...], jnp.concatenate([win] * 3, axis=0), NT)
    high = part.astype(BF16).astype(F32)
    lane = lax.broadcasted_iota(jnp.int32, part.shape, 1)
    part = jnp.where((lane >= width) & (lane < 2 * width), part - high, high).astype(BF16)
    field = dot(part, ru3[...], NN)
    centre = field[:, :nlon]
    image = (
        balance[0] * centre[:nlat]
        + balance[1] * pltpu.roll(field, wide - 1, 1)[:nlat, :nlon]
        + balance[2] * pltpu.roll(field, 1, 1)[:nlat, :nlon]
        + balance[3] * pltpu.roll(centre, tall - 1, 0)[:nlat]
        + balance[4] * pltpu.roll(centre, 1, 0)[:nlat]
    )
    misfit = weight * (image - inn)

    def longer(value):
        return jnp.concatenate([value, jnp.zeros((value.shape[0], wide - nlon), F32)], axis=1)

    def taller(value):
        return jnp.concatenate([value, jnp.zeros((tall - nlat, value.shape[1]), F32)], axis=0)

    across = (
        longer(balance[0] * misfit)
        + pltpu.roll(longer(balance[1] * misfit), 1, 1)
        + pltpu.roll(longer(balance[2] * misfit), wide - 1, 1)
    )
    along = pltpu.roll(taller(balance[3] * misfit), 1, 0) + pltpu.roll(taller(balance[4] * misfit), tall - 1, 0)
    grad = taller(across) + longer(along)
    back = dot(three(grad, 1), rub3[...], NT).T
    high, low = split(back)
    return dot(high, rl_hi[...], NN) + (dot(high, rl_lo[...], NN) + dot(low, rl_hi[...], NN))


def fine_kernel(bands, band_ref, *refs):
    wins, (inn, weight), consts = refs[:bands], refs[bands : bands + 2], refs[bands + 2 : bands + 8]
    outs, window = refs[bands + 8 : -1], refs[-1]
    turn, level = pl.program_id(0), pl.program_id(1)
    width = wins[0].shape[1]
    for s in range(bands):

        @pl.when(turn == s)
        def _():
            window[:width, :] = wins[s][level]

    if width < window.shape[0]:
        window[width:, :] = jnp.zeros((window.shape[0] - width, window.shape[1]), F32)
    result = fine_level(window[...], inn[0], weight[0], *consts)
    for s in range(bands):

        @pl.when(turn == s)
        def _():
            outs[s][level] = result[:width]


def add_kernel(bands, band_ref, ctrl, *refs):
    pieces, out = refs[:bands], refs[-1]
    band = band_ref[0]
    for s in range(bands):
        owner = lax.rem(band - s + bands, bands)
        out[0, owner, 0] = ctrl[0, owner, 0] + pieces[s][0, 0]


def scalar_grid(grid, in_specs, out_specs, scratch=()):
    return pltpu.PrefetchScalarGridSpec(
        num_scalar_prefetch=1, grid=grid, in_specs=in_specs, out_specs=out_specs, scratch_shapes=scratch
    )


def whole_block(array):
    return pl.BlockSpec(array.shape, lambda *ids: (0,) * len(array.shape))


def chunks_of(owned):
    count = math.gcd(owned, 4)
    return [(owned // count * i, owned // count) for i in range(count)]


def body(controls, members, loc_lon, loc_lat, balance, innovation, obs_weight):
    bands, mates = lax.axis_size("band"), lax.axis_size("member")
    band = lax.axis_index("band")
    band_array = jnp.reshape(band, (1,)).astype(jnp.int32)
    held, levels, cy, nx = controls.shape
    ny = loc_lat.shape[0]
    cx = nx // mates
    owned = levels // bands
    width, deep = round_up(cx + 4, 8), round_up(cx + 4, 16)
    lanes = min(round_up(cy + 4, 128), ny)
    nlat, nlon = innovation.shape[1:]
    tall, wide = nlat + 8, round_up(nlon + 2, 128)
    scale = 1.0 / math.sqrt(held * mates - 1)

    turned = jnp.roll(loc_lat, (-cy * band, -cy * band), (0, 1))
    lat3, lat_t3 = outer_three(turned, 1), outer_three(turned.T, 1)
    lon3, lon_b3 = outer_three(loc_lon, 1), outer_three(loc_lon, 0)
    ru = jnp.asarray(edged_matrix(cx, wide, deep).T)
    ru3, rub3 = outer_three(ru, 0), outer_three(ru, 1)
    row = lax.broadcasted_iota(jnp.int32, (tall, lanes), 0)
    col = lax.broadcasted_iota(jnp.int32, (tall, lanes), 1)
    first, last = band == 0, band == bands - 1
    off = (first & ((row == tall - 1) | (col < 2))) | (last & ((row == nlat) | (col >= cy + 2)))
    rl = jnp.where(off, 0.0, jnp.asarray(edged_matrix(cy, tall, lanes)))
    rl3, (rl_hi, rl_lo) = outer_three(rl, 1), outer_split(rl)

    plan = chunks_of(owned)
    count = plan[0][1]
    ctrl_view = controls.reshape(held, bands, owned, cy, nx)
    mem_view = members.reshape(held, bands, owned, cy, nx)
    wrap_scratch = pltpu.VMEM((nx + 16, ny), F32)

    def shifted(value, s):
        if s % bands == 0:
            return value
        return lax.ppermute(value, "band", [(i, (i + s) % bands) for i in range(bands)])

    def sent(views, first_level, s):
        at = lax.rem(band - s + bands, bands)
        size, start = (held, 1, count, cy, nx), (0, at, first_level, 0, 0)
        return jnp.stack([lax.dynamic_slice(v, start, size)[:, 0] for v in views])

    def received(views, first_level):
        return [shifted(sent(views, first_level, s), -s) for s in range(1, bands)]

    def own_spec(first_level):
        return pl.BlockSpec((held, None, None, cy, nx), lambda l, b: (0, b[0], first_level + l, 0, 0))

    def piece_spec(at):
        return pl.BlockSpec((None, held, None, cy, nx), lambda l, b: (at, 0, l, 0, 0))

    def swapped_spec(parts):
        return pl.BlockSpec((mates, parts, None, width, ny), lambda l, b: (0, 0, l, 0, 0))

    def small_spec(parts):
        return pl.BlockSpec((parts, None, width, lanes), lambda l, b: (0, l, 0, 0))

    def stage_in(first_level, pieces, coarse):
        arrays, specs = [], []
        if pieces is not None:
            for at, view in enumerate((ctrl_view, mem_view)):
                arrays += [view] + [p[0] for p in pieces[at]]
                specs += [own_spec(first_level)] + [piece_spec(p[1]) for p in pieces[at]]
            arrays += [lat3, lon3]
            specs += [whole_block(lat3), whole_block(lon3)]
        if coarse is not None:
            last = coarse[0].shape[0] - 1
            arrays += coarse
            specs += [pl.BlockSpec((None, None, width, lanes), lambda l, b: (last, l, 0, 0))] * bands
        parts = (pieces is not None) + (coarse is not None)

        def kernel(band_ref, *refs):
            refs = list(refs)
            wrapped, out = refs.pop(), refs.pop()
            if pieces is not None:
                fields_of(scale, refs[:bands], refs[bands : 2 * bands], *refs[2 * bands : 2 * bands + 2], wrapped, out)
            if coarse is not None:
                overlapped(cy, refs[-bands:], out)

        return pl.pallas_call(
            kernel,
            grid_spec=scalar_grid((count,), specs, swapped_spec(parts), [wrap_scratch]),
            out_shape=jax.ShapeDtypeStruct((mates, parts, count, width, ny), F32),
            name="stage_in",
        )(band_array, *arrays)

    def stage_out(swapped, fine_out):
        arrays, specs = [swapped], [swapped_spec(swapped.shape[1])]
        parts = 1 + (fine_out is not None)
        if fine_out is not None:
            arrays += fine_out
            specs += [pl.BlockSpec((None, None, width, lanes), lambda l, b: (0, l, 0, 0))] * bands

        def kernel(band_ref, *refs):
            outs = refs[len(arrays) :]
            windows_of(cy, refs[0], outs)
            if fine_out is not None:
                for s in range(bands):
                    outs[s][1] = refs[1 + (bands - s) % bands][...]

        return pl.pallas_call(
            kernel,
            grid_spec=scalar_grid((count,), specs, [small_spec(parts)] * bands),
            out_shape=[jax.ShapeDtypeStruct((parts, count, width, lanes), F32)] * bands,
            name="stage_out",
        )(band_array, *arrays)

    def adjoint(swapped, first_level, perts):
        arrays = [swapped, mem_view] + [p[0] for p in perts] + [lat_t3, lon_b3]
        specs = [swapped_spec(swapped.shape[1]), own_spec(first_level)] + [piece_spec(p[1]) for p in perts]
        specs += [whole_block(lat_t3), whole_block(lon_b3)]

        def kernel(band_ref, swap_ref, *refs):
            adjoint_of(scale, swap_ref, refs[:bands], *refs[bands : bands + 2], refs[-1], refs[bands + 2 : -1])

        return pl.pallas_call(
            kernel,
            grid_spec=scalar_grid(
                (count,),
                specs,
                [pl.BlockSpec((held, None, cy, nx), lambda l, b: (0, l, 0, 0))] * bands,
                [wrap_scratch],
            ),
            out_shape=[jax.ShapeDtypeStruct((held, count, cy, nx), F32)] * bands,
            name="adjoint",
        )(band_array, *arrays)

    def fine(wins, first_level):
        def level(o, l, b):
            return (lax.rem(b[0] - o + bands, bands) * owned + first_level + l, 0, 0)

        consts = (balance, rl3, ru3, rl_hi, rl_lo, rub3)
        return pl.pallas_call(
            functools.partial(fine_kernel, bands),
            grid_spec=scalar_grid(
                (bands, count),
                [pl.BlockSpec((None, count, width, lanes), lambda o, l, b: (0, 0, 0, 0))] * bands
                + [pl.BlockSpec((1, nlat, nlon), level)] * 2
                + [whole_block(c) for c in consts],
                [pl.BlockSpec((None, count, width, lanes), lambda o, l, b: (0, 0, 0, 0))] * bands,
                [pltpu.VMEM((deep, lanes), F32)],
            ),
            out_shape=[jax.ShapeDtypeStruct((1, count, width, lanes), F32)] * bands,
            name="fine",
        )(band_array, *wins, innovation, obs_weight, *consts)

    def added(result, pieces, first_level):
        block = pl.BlockSpec((1, bands, 1, cy, nx), lambda k, l, b: (k, 0, first_level + l, 0, 0))
        piece = pl.BlockSpec((1, 1, cy, nx), lambda k, l, b: (k, l, 0, 0))
        carried = [] if result is None else [result]
        return pl.pallas_call(
            functools.partial(add_kernel, bands),
            grid_spec=scalar_grid(
                (held, count),
                [block] + [piece] * bands + [pl.BlockSpec(memory_space=pl.ANY)] * len(carried),
                block,
            ),
            out_shape=jax.ShapeDtypeStruct(ctrl_view.shape, F32),
            input_output_aliases={2 + bands: 0} if carried else {},
            name="added",
        )(band_array, ctrl_view, *pieces, *carried)

    swap = functools.partial(lax.all_to_all, split_axis=0, concat_axis=0, tiled=True)
    total = len(plan)
    pieces, small, result = [], None, None
    for i, (first, _) in enumerate(plan):
        if i == 0:
            sides = []
            for view in (ctrl_view, mem_view):
                sides.append([(p, 0) for p in received((view,), first)])
        else:
            pair = received((ctrl_view, mem_view), first)
            sides = [[(p, 0) for p in pair], [(p, 1) for p in pair]]
        pieces.append(sides)
    for t in range(total + 2):
        now, middle, old = (i if 0 <= i < total else None for i in (t, t - 1, t - 2))
        level = None if now is None else plan[now][0]
        coarse = None if old is None else [small[(bands - s) % bands] for s in range(bands)]
        value = None
        if now is not None or old is not None:
            value = stage_in(level, None if now is None else pieces[now], coarse)
        if value is not None:
            value = swap(value, "member")
        fine_out = None
        if middle is not None:
            fine_out = fine(small, plan[middle][0])
        sending = None
        if now is not None:
            sending = stage_out(value, fine_out)
        elif fine_out is not None:
            sending = [fine_out[(bands - s) % bands] for s in range(bands)]
        if sending is not None:
            small = [shifted(p, s) for s, p in enumerate(sending)]
        if old is not None:
            back = adjoint(value, plan[old][0], pieces[old][1])
            back = [shifted(p, s) for s, p in enumerate(back)]
            result = added(result, back, plan[old][0])
    return result.reshape(controls.shape)


def solution(mesh):
    return jax.shard_map(
        body,
        mesh=mesh,
        in_specs=(
            P("member", None, "band", None),
            P("member", None, "band", None),
            P(),
            P(),
            P(None, "band", "member"),
            P(None, "band", "member"),
            P(None, "band", "member"),
        ),
        out_specs=P("member", None, "band", None),
        check_vma=False,
    )
```

```python
import functools
import math

import jax
import jax.numpy as jnp
import numpy as np
from jax import lax
from jax.experimental import pallas as pl
from jax.experimental.pallas import tpu as pltpu
from jax.sharding import PartitionSpec as P


F32, BF16 = jnp.float32, jnp.bfloat16
phase_fraction = (0.625, 0.875, 0.125, 0.375)
phase_start = (0, 0, 1, 1)
NN = (((1,), (0,)), ((), ()))
NT = (((1,), (1,)), ((), ()))


def cubic_weights(fraction):
    return (
        (-(fraction**3) + 2 * fraction**2 - fraction) / 2,
        (3 * fraction**3 - 5 * fraction**2 + 2) / 2,
        (-3 * fraction**3 + 4 * fraction**2 + fraction) / 2,
        (fraction**3 - fraction**2) / 2,
    )


def round_up(value, step):
    return -(-value // step) * step


def edged_matrix(coarse, rows_out, cols_out):
    matrix = np.zeros((rows_out, cols_out), np.float32)
    fine = 4 * coarse
    for row, at in [(i, i) for i in range(fine + 1)] + [(-1, rows_out - 1)]:
        cell, phase = divmod(row, 4)
        for tap, weight in enumerate(cubic_weights(phase_fraction[phase])):
            matrix[at, cell + phase_start[phase] + tap] += weight
    return matrix


def split(value):
    high = value.astype(BF16)
    return high, (value - high.astype(F32)).astype(BF16)


def outer_split(value):
    high = lax.reduce_precision(value, 8, 7)
    return high.astype(BF16), lax.reduce_precision(value - high, 8, 7).astype(BF16)


def three(value, axis):
    high, low = split(value)
    return jnp.concatenate([high, low, high], axis=axis)


def outer_three(value, axis):
    high, low = outer_split(value)
    return jnp.concatenate([high, high, low], axis=axis)


def dot(left, right, dims):
    return lax.dot_general(left, right, dims, preferred_element_type=F32)


def field_of(ctrls, lat, lon, k):
    ctrl = jnp.concatenate([p[k] for p in ctrls], axis=0)
    rowwise = dot(three(ctrl, 1), lon[...], NT)
    return dot(lat[...], three(rowwise, 0), NN)


def increment_of(scale, field, perts, wrapped, out):
    nx = wrapped.shape[0] - 16
    total = None
    for k in range(perts[0].shape[0]):
        product = jnp.concatenate([p[k] for p in perts], axis=0) * field(k)
        total = product if total is None else total + product
    wrapped[8 : 8 + nx, :] = (total * scale).T
    wrapped[0:8, :] = wrapped[nx : nx + 8, :]
    wrapped[nx + 8 : nx + 16, :] = wrapped[8:16, :]
    windows, _, width, _ = out.shape
    step = nx // windows
    for m in range(windows):
        out[m, 0] = wrapped[step * m + 6 : step * m + 6 + width, :]


def overlapped(stripe, parts, out):
    windows, _, width, lats = out.shape
    total = None
    for s, part in enumerate(parts):
        window = part[...] if part.shape[0] == width else unpacked(stripe, part[...], True)
        grown = jnp.concatenate([window, jnp.zeros((width, lats - window.shape[1]), F32)], axis=1)
        turned = pltpu.roll(grown, (stripe * s - 2) % lats, 1)
        total = turned if total is None else total + turned
    for m in range(windows):
        out[m, out.shape[1] - 1] = total


def packed(stripe, window, result):
    lanes = window.shape[1]
    lane = lax.broadcasted_iota(jnp.int32, window.shape, 1)
    low = jnp.where(lane < stripe, window, pltpu.roll(result, stripe, 1))
    edge = jnp.where(lane < stripe + 4, window, pltpu.roll(result, 4, 1))
    edge = jnp.concatenate([edge, jnp.zeros((lanes - edge.shape[0], lanes), F32)], axis=0)
    return jnp.concatenate([low, edge.T[stripe : stripe + 8]], axis=0)


def unpacked(stripe, value, second):
    width, lanes = value.shape[0] - 8, value.shape[1]
    low, edge = value[:width], value[width:]
    edge = jnp.concatenate([edge, jnp.zeros((lanes - 8, lanes), F32)], axis=0).T[:width]
    lane = lax.broadcasted_iota(jnp.int32, low.shape, 1)
    if second:
        return jnp.where(lane < stripe, pltpu.roll(low, lanes - stripe, 1), pltpu.roll(edge, stripe - 4, 1))
    return jnp.where(lane < stripe, low, pltpu.roll(edge, stripe, 1))


def windows_of(stripe, parts):
    total = parts[0, 0]
    for m in range(1, parts.shape[0]):
        total = total + parts[m, 0]
    lats = total.shape[1]
    return [pltpu.roll(total, (2 - stripe * s) % lats, 1) for s in range(lats // stripe)]


def adjoint_of(scale, grads, perts, lat, lon, wrapped, outs):
    stripe = perts[0].shape[1]
    nx = lon.shape[1]
    wrapped[...] = jnp.zeros_like(wrapped)
    windows, parts, width, _ = grads.shape
    step = nx // windows
    for m in range(windows):
        place = slice(step * m + 6, step * m + 6 + width)
        wrapped[place, :] = wrapped[place, :] + grads[m, parts - 1]
    wrapped[nx : nx + 8, :] = wrapped[nx : nx + 8, :] + wrapped[0:8, :]
    wrapped[8:16, :] = wrapped[8:16, :] + wrapped[nx + 8 : nx + 16, :]
    grad = wrapped[8 : 8 + nx, :].T * scale
    for k in range(perts[0].shape[0]):
        weighted = jnp.concatenate([p[k] for p in perts], axis=0) * grad
        half = dot(lat[...], three(weighted, 0), NN)
        result = dot(three(half, 1), lon[...], NN)
        for s, out in enumerate(outs):
            out[k] = result[stripe * s : stripe * (s + 1), :]


def fine_level(window, inn, weight, balance, rl3, ru3, rl_hi, rl_lo, rub3):
    nlat, nlon = inn.shape
    tall, wide = rl3.shape[0], ru3.shape[1]
    width = window.shape[0]
    win = three(window, 1)
    part = dot(rl3[...], jnp.concatenate([win] * 3, axis=0), NT)
    high = part.astype(BF16).astype(F32)
    lane = lax.broadcasted_iota(jnp.int32, part.shape, 1)
    part = jnp.where((lane >= width) & (lane < 2 * width), part - high, high).astype(BF16)
    field = dot(part, ru3[...], NN)
    centre = field[:, :nlon]
    image = (
        balance[0] * centre[:nlat]
        + balance[1] * pltpu.roll(field, wide - 1, 1)[:nlat, :nlon]
        + balance[2] * pltpu.roll(field, 1, 1)[:nlat, :nlon]
        + balance[3] * pltpu.roll(centre, tall - 1, 0)[:nlat]
        + balance[4] * pltpu.roll(centre, 1, 0)[:nlat]
    )
    misfit = weight * (image - inn)

    def longer(value):
        return jnp.concatenate([value, jnp.zeros((value.shape[0], wide - nlon), F32)], axis=1)

    def taller(value):
        return jnp.concatenate([value, jnp.zeros((tall - nlat, value.shape[1]), F32)], axis=0)

    across = (
        longer(balance[0] * misfit)
        + pltpu.roll(longer(balance[1] * misfit), 1, 1)
        + pltpu.roll(longer(balance[2] * misfit), wide - 1, 1)
    )
    along = pltpu.roll(taller(balance[3] * misfit), 1, 0) + pltpu.roll(taller(balance[4] * misfit), tall - 1, 0)
    grad = taller(across) + longer(along)
    back = dot(three(grad, 1), rub3[...], NT).T
    high, low = split(back)
    return dot(high, rl_hi[...], NN) + (dot(high, rl_lo[...], NN) + dot(low, rl_hi[...], NN))


def fine_kernel(bands, stripe, band_ref, *refs):
    wins, (inn, weight), consts = refs[:bands], refs[bands : bands + 2], refs[bands + 2 : bands + 8]
    outs, window = refs[bands + 8 : -1], refs[-1]
    turn, level = pl.program_id(0), pl.program_id(1)
    width = outs[0].shape[1]
    for s in range(bands):

        @pl.when(turn == s)
        def _():
            value = wins[s][level]
            window[:width, :] = value if value.shape[0] == width else unpacked(stripe, value, False)

    if width < window.shape[0]:
        window[width:, :] = jnp.zeros((window.shape[0] - width, window.shape[1]), F32)
    result = fine_level(window[...], inn[0], weight[0], *consts)
    for s in range(bands):

        @pl.when(turn == s)
        def _():
            outs[s][level] = result[:width]


def add_kernel(bands, band_ref, ctrl, *refs):
    pieces, out = refs[:bands], refs[-1]
    band = band_ref[0]
    for s in range(bands):
        owner = lax.rem(band - s + bands, bands)
        out[0, owner, 0] = ctrl[0, owner, 0] + pieces[s][0, 0]


def scalar_grid(grid, in_specs, out_specs, scratch=()):
    return pltpu.PrefetchScalarGridSpec(
        num_scalar_prefetch=1, grid=grid, in_specs=in_specs, out_specs=out_specs, scratch_shapes=scratch
    )


def whole_block(array):
    return pl.BlockSpec(array.shape, lambda *ids: (0,) * len(array.shape))


def chunks_of(owned):
    count = math.gcd(owned, 4)
    return [(owned // count * i, owned // count) for i in range(count)]


def body(controls, members, loc_lon, loc_lat, balance, innovation, obs_weight):
    bands, mates = lax.axis_size("band"), lax.axis_size("member")
    band = lax.axis_index("band")
    band_array = jnp.reshape(band, (1,)).astype(jnp.int32)
    held, levels, cy, nx = controls.shape
    ny = loc_lat.shape[0]
    cx = nx // mates
    owned = levels // bands
    width, deep = round_up(cx + 4, 8), round_up(cx + 4, 16)
    lanes = min(round_up(cy + 4, 128), ny)
    nlat, nlon = innovation.shape[1:]
    tall, wide = nlat + 8, round_up(nlon + 2, 128)
    scale = 1.0 / math.sqrt(held * mates - 1)

    turned = jnp.roll(loc_lat, (-cy * band, -cy * band), (0, 1))
    lat3, lat_t3 = outer_three(turned, 1), outer_three(turned.T, 1)
    lon3, lon_b3 = outer_three(loc_lon, 1), outer_three(loc_lon, 0)
    ru = jnp.asarray(edged_matrix(cx, wide, deep).T)
    ru3, rub3 = outer_three(ru, 0), outer_three(ru, 1)
    row = lax.broadcasted_iota(jnp.int32, (tall, lanes), 0)
    col = lax.broadcasted_iota(jnp.int32, (tall, lanes), 1)
    first, last = band == 0, band == bands - 1
    off = (first & ((row == tall - 1) | (col < 2))) | (last & ((row == nlat) | (col >= cy + 2)))
    rl = jnp.where(off, 0.0, jnp.asarray(edged_matrix(cy, tall, lanes)))
    rl3, (rl_hi, rl_lo) = outer_three(rl, 1), outer_split(rl)

    plan = chunks_of(owned)
    count = plan[0][1]
    ctrl_view = controls.reshape(held, bands, owned, cy, nx)
    mem_view = members.reshape(held, bands, owned, cy, nx)
    wrap_scratch = pltpu.VMEM((nx + 16, ny), F32)

    def shifted(value, s):
        if s % bands == 0:
            return value
        return lax.ppermute(value, "band", [(i, (i + s) % bands) for i in range(bands)])

    def sent(views, first_level, s):
        at = lax.rem(band - s + bands, bands)
        size, start = (held, 1, count, cy, nx), (0, at, first_level, 0, 0)
        return jnp.stack([lax.dynamic_slice(v, start, size)[:, 0] for v in views])

    def received(views, first_level):
        return [shifted(sent(views, first_level, s), -s) for s in range(1, bands)]

    def own_spec(first_level):
        return pl.BlockSpec((held, None, None, cy, nx), lambda l, b: (0, b[0], first_level + l, 0, 0))

    def piece_spec(at):
        return pl.BlockSpec((None, held, None, cy, nx), lambda l, b: (at, 0, l, 0, 0))

    def swapped_spec(parts):
        return pl.BlockSpec((mates, parts, None, width, ny), lambda l, b: (0, 0, l, 0, 0))

    def operands(view, first_level, pieces):
        specs = [own_spec(first_level)] + [piece_spec(p[1]) for p in pieces]
        return [view] + [p[0] for p in pieces], specs

    field_spec = pl.BlockSpec((held, None, ny, nx), lambda l, b: (0, l, 0, 0))

    def fields(first_level, pieces):
        arrays, specs = operands(ctrl_view, first_level, pieces)

        def kernel(band_ref, *refs):
            for k in range(held):
                refs[-1][k] = field_of(refs[:bands], *refs[bands : bands + 2], k)

        return pl.pallas_call(
            kernel,
            grid_spec=scalar_grid((count,), specs + [whole_block(lat3), whole_block(lon3)], field_spec),
            out_shape=jax.ShapeDtypeStruct((held, count, ny, nx), F32),
            name="fields",
        )(band_array, *arrays, lat3, lon3)

    def stage_in(first_level, pieces, ready, coarse):
        arrays, specs = [], []
        if pieces is not None:
            arrays, specs = operands(mem_view, first_level, pieces[1])
            if ready is not None:
                arrays, specs = arrays + [ready], specs + [field_spec]
            else:
                more, more_specs = operands(ctrl_view, first_level, pieces[0])
                arrays += more + [lat3, lon3]
                specs += more_specs + [whole_block(lat3), whole_block(lon3)]
        if coarse is not None:
            last = coarse[0].shape[0] - 1
            arrays += coarse
            specs += [pl.BlockSpec((None, None, coarse[0].shape[2], lanes), lambda l, b: (last, l, 0, 0))] * bands
        parts = (pieces is not None) + (coarse is not None)

        def kernel(band_ref, *refs):
            refs = list(refs)
            wrapped, out = refs.pop(), refs.pop()
            if pieces is not None:
                if ready is not None:
                    field = lambda k: refs[bands][k]
                else:
                    field = functools.partial(field_of, refs[bands : 2 * bands], *refs[2 * bands : 2 * bands + 2])
                increment_of(scale, field, refs[:bands], wrapped, out)
            if coarse is not None:
                overlapped(cy, refs[-bands:], out)

        return pl.pallas_call(
            kernel,
            grid_spec=scalar_grid((count,), specs, swapped_spec(parts), [wrap_scratch]),
            out_shape=jax.ShapeDtypeStruct((mates, parts, count, width, ny), F32),
            name="stage_in",
        )(band_array, *arrays)

    def stage_out(swapped, fine_out):
        arrays, specs = [swapped], [swapped_spec(swapped.shape[1])]
        joined = fine_out is not None
        tight = joined and 2 * cy == lanes
        parts, high = (1, width + 8) if tight else (1 + joined, width)
        if joined:
            arrays += fine_out
            specs += [pl.BlockSpec((None, None, width, lanes), lambda l, b: (0, l, 0, 0))] * bands

        def kernel(band_ref, *refs):
            outs = refs[len(arrays) :]
            for s, window in enumerate(windows_of(cy, refs[0])):
                window = window[:, :lanes]
                result = refs[1 + (bands - s) % bands][...] if joined else None
                if tight:
                    outs[s][0] = packed(cy, window, result)
                else:
                    outs[s][0] = window
                    if joined:
                        outs[s][1] = result

        return pl.pallas_call(
            kernel,
            grid_spec=scalar_grid(
                (count,), specs, [pl.BlockSpec((parts, None, high, lanes), lambda l, b: (0, l, 0, 0))] * bands
            ),
            out_shape=[jax.ShapeDtypeStruct((parts, count, high, lanes), F32)] * bands,
            name="stage_out",
        )(band_array, *arrays)

    def adjoint(swapped, first_level, perts):
        arrays = [swapped, mem_view] + [p[0] for p in perts] + [lat_t3, lon_b3]
        specs = [swapped_spec(swapped.shape[1]), own_spec(first_level)] + [piece_spec(p[1]) for p in perts]
        specs += [whole_block(lat_t3), whole_block(lon_b3)]

        def kernel(band_ref, swap_ref, *refs):
            adjoint_of(scale, swap_ref, refs[:bands], *refs[bands : bands + 2], refs[-1], refs[bands + 2 : -1])

        return pl.pallas_call(
            kernel,
            grid_spec=scalar_grid(
                (count,),
                specs,
                [pl.BlockSpec((held, None, cy, nx), lambda l, b: (0, l, 0, 0))] * bands,
                [wrap_scratch],
            ),
            out_shape=[jax.ShapeDtypeStruct((held, count, cy, nx), F32)] * bands,
            name="adjoint",
        )(band_array, *arrays)

    def fine(wins, first_level):
        def level(o, l, b):
            return (lax.rem(b[0] - o + bands, bands) * owned + first_level + l, 0, 0)

        consts = (balance, rl3, ru3, rl_hi, rl_lo, rub3)
        return pl.pallas_call(
            functools.partial(fine_kernel, bands, cy),
            grid_spec=scalar_grid(
                (bands, count),
                [pl.BlockSpec((None, count, wins[0].shape[2], lanes), lambda o, l, b: (0, 0, 0, 0))] * bands
                + [pl.BlockSpec((1, nlat, nlon), level)] * 2
                + [whole_block(c) for c in consts],
                [pl.BlockSpec((None, count, width, lanes), lambda o, l, b: (0, 0, 0, 0))] * bands,
                [pltpu.VMEM((deep, lanes), F32)],
            ),
            out_shape=[jax.ShapeDtypeStruct((1, count, width, lanes), F32)] * bands,
            name="fine",
        )(band_array, *wins, innovation, obs_weight, *consts)

    def added(result, pieces, first_level):
        block = pl.BlockSpec((1, bands, 1, cy, nx), lambda k, l, b: (k, 0, first_level + l, 0, 0))
        piece = pl.BlockSpec((1, 1, cy, nx), lambda k, l, b: (k, l, 0, 0))
        carried = [] if result is None else [result]
        return pl.pallas_call(
            functools.partial(add_kernel, bands),
            grid_spec=scalar_grid(
                (held, count),
                [block] + [piece] * bands + [pl.BlockSpec(memory_space=pl.ANY)] * len(carried),
                block,
            ),
            out_shape=jax.ShapeDtypeStruct(ctrl_view.shape, F32),
            input_output_aliases={2 + bands: 0} if carried else {},
            name="added",
        )(band_array, ctrl_view, *pieces, *carried)

    swap = functools.partial(lax.all_to_all, split_axis=0, concat_axis=0, tiled=True)
    total = len(plan)
    pieces, small, result = [], None, None
    for i, (first, _) in enumerate(plan):
        if i in (0, total - 1):
            sides = []
            for view in (ctrl_view, mem_view):
                sides.append([(p, 0) for p in received((view,), first)])
        else:
            pair = received((ctrl_view, mem_view), first)
            sides = [[(p, 0) for p in pair], [(p, 1) for p in pair]]
        pieces.append(sides)
    for t in range(total + 2):
        now, middle, old = (i if 0 <= i < total else None for i in (t, t - 1, t - 2))
        level = None if now is None else plan[now][0]
        ready = None
        if now == total - 1:
            ready = fields(level, pieces[now][0])
        coarse = None if old is None else [small[(bands - s) % bands] for s in range(bands)]
        value = None
        if now is not None or old is not None:
            value = stage_in(level, None if now is None else pieces[now], ready, coarse)
        if value is not None:
            value = swap(value, "member")
        fine_out = None
        if middle is not None:
            fine_out = fine(small, plan[middle][0])
        sending = None
        if now is not None:
            sending = stage_out(value, fine_out)
        elif fine_out is not None:
            sending = [fine_out[(bands - s) % bands] for s in range(bands)]
        if sending is not None:
            small = [shifted(p, s) for s, p in enumerate(sending)]
        if old is not None:
            back = adjoint(value, plan[old][0], pieces[old][1])
            back = [shifted(p, s) for s, p in enumerate(back)]
            result = added(result, back, plan[old][0])
    return result.reshape(controls.shape)


def solution(mesh):
    return jax.shard_map(
        body,
        mesh=mesh,
        in_specs=(
            P("member", None, "band", None),
            P("member", None, "band", None),
            P(),
            P(),
            P(None, "band", "member"),
            P(None, "band", "member"),
            P(None, "band", "member"),
        ),
        out_specs=P("member", None, "band", None),
        check_vma=False,
    )
```

```python
import functools
import math

import jax
import jax.numpy as jnp
import numpy as np
from jax import lax
from jax.experimental import pallas as pl
from jax.experimental.pallas import tpu as pltpu
from jax.sharding import PartitionSpec as P


F32, BF16 = jnp.float32, jnp.bfloat16
phase_fraction = (0.625, 0.875, 0.125, 0.375)
phase_start = (0, 0, 1, 1)
NN = (((1,), (0,)), ((), ()))
NT = (((1,), (1,)), ((), ()))


def cubic_weights(fraction):
    return (
        (-(fraction**3) + 2 * fraction**2 - fraction) / 2,
        (3 * fraction**3 - 5 * fraction**2 + 2) / 2,
        (-3 * fraction**3 + 4 * fraction**2 + fraction) / 2,
        (fraction**3 - fraction**2) / 2,
    )


def round_up(value, step):
    return -(-value // step) * step


def edged_matrix(coarse, rows_out, cols_out):
    matrix = np.zeros((rows_out, cols_out), np.float32)
    fine = 4 * coarse
    for row, at in [(i, i) for i in range(fine + 1)] + [(-1, rows_out - 1)]:
        cell, phase = divmod(row, 4)
        for tap, weight in enumerate(cubic_weights(phase_fraction[phase])):
            matrix[at, cell + phase_start[phase] + tap] += weight
    return matrix


def split(value):
    high = value.astype(BF16)
    return high, (value - high.astype(F32)).astype(BF16)


def outer_split(value):
    high = lax.reduce_precision(value, 8, 7)
    return high.astype(BF16), lax.reduce_precision(value - high, 8, 7).astype(BF16)


def three(value, axis):
    high, low = split(value)
    return jnp.concatenate([high, low, high], axis=axis)


def outer_three(value, axis):
    high, low = outer_split(value)
    return jnp.concatenate([high, high, low], axis=axis)


def dot(left, right, dims):
    return lax.dot_general(left, right, dims, preferred_element_type=F32)


def field_of(ctrls, lat, lon, k):
    ctrl = jnp.concatenate([p[k] for p in ctrls], axis=0)
    rowwise = dot(three(ctrl, 1), lon[...], NT)
    return dot(lat[...], three(rowwise, 0), NN)


def increment_of(scale, field, perts, wrapped, out):
    nx = wrapped.shape[0] - 16
    total = None
    for k in range(perts[0].shape[0]):
        product = jnp.concatenate([p[k] for p in perts], axis=0) * field(k)
        total = product if total is None else total + product
    wrapped[8 : 8 + nx, :] = (total * scale).T
    wrapped[0:8, :] = wrapped[nx : nx + 8, :]
    wrapped[nx + 8 : nx + 16, :] = wrapped[8:16, :]
    windows, _, width, _ = out.shape
    step = nx // windows
    for m in range(windows):
        out[m, 0] = wrapped[step * m + 6 : step * m + 6 + width, :]


def overlapped(stripe, parts, out):
    windows, _, width, lats = out.shape
    total = None
    for s, part in enumerate(parts):
        window = part[...] if part.shape[0] == width else unpacked(stripe, part[...], True)
        grown = jnp.concatenate([window, jnp.zeros((width, lats - window.shape[1]), F32)], axis=1)
        turned = pltpu.roll(grown, (stripe * s - 2) % lats, 1)
        total = turned if total is None else total + turned
    for m in range(windows):
        out[m, out.shape[1] - 1] = total


def packed(stripe, window, result):
    lanes = window.shape[1]
    lane = lax.broadcasted_iota(jnp.int32, window.shape, 1)
    low = jnp.where(lane < stripe, window, pltpu.roll(result, stripe, 1))
    edge = jnp.where(lane < stripe + 4, window, pltpu.roll(result, 4, 1))
    edge = jnp.concatenate([edge, jnp.zeros((lanes - edge.shape[0], lanes), F32)], axis=0)
    return jnp.concatenate([low, edge.T[stripe : stripe + 8]], axis=0)


def unpacked(stripe, value, second):
    width, lanes = value.shape[0] - 8, value.shape[1]
    low, edge = value[:width], value[width:]
    edge = jnp.concatenate([edge, jnp.zeros((lanes - 8, lanes), F32)], axis=0).T[:width]
    lane = lax.broadcasted_iota(jnp.int32, low.shape, 1)
    if second:
        return jnp.where(lane < stripe, pltpu.roll(low, lanes - stripe, 1), pltpu.roll(edge, stripe - 4, 1))
    return jnp.where(lane < stripe, low, pltpu.roll(edge, stripe, 1))


def windows_of(stripe, parts):
    total = parts[0, 0]
    for m in range(1, parts.shape[0]):
        total = total + parts[m, 0]
    lats = total.shape[1]
    return [pltpu.roll(total, (2 - stripe * s) % lats, 1) for s in range(lats // stripe)]


def adjoint_of(scale, grads, perts, lat, lon, wrapped, outs):
    stripe = perts[0].shape[1]
    nx = lon.shape[1]
    wrapped[...] = jnp.zeros_like(wrapped)
    windows, parts, width, _ = grads.shape
    step = nx // windows
    for m in range(windows):
        place = slice(step * m + 6, step * m + 6 + width)
        wrapped[place, :] = wrapped[place, :] + grads[m, parts - 1]
    wrapped[nx : nx + 8, :] = wrapped[nx : nx + 8, :] + wrapped[0:8, :]
    wrapped[8:16, :] = wrapped[8:16, :] + wrapped[nx + 8 : nx + 16, :]
    grad = wrapped[8 : 8 + nx, :].T * scale
    for k in range(perts[0].shape[0]):
        weighted = jnp.concatenate([p[k] for p in perts], axis=0) * grad
        half = dot(lat[...], three(weighted, 0), NN)
        result = dot(three(half, 1), lon[...], NN)
        for s, out in enumerate(outs):
            out[k] = result[stripe * s : stripe * (s + 1), :]


def fine_level(window, inn, weight, balance, rl3, ru3, rl_hi, rl_lo, rub3):
    nlat, nlon = inn.shape
    tall, wide = rl3.shape[0], ru3.shape[1]
    width = window.shape[0]
    win = three(window, 1)
    part = dot(rl3[...], jnp.concatenate([win] * 3, axis=0), NT)
    high = part.astype(BF16).astype(F32)
    lane = lax.broadcasted_iota(jnp.int32, part.shape, 1)
    part = jnp.where((lane >= width) & (lane < 2 * width), part - high, high).astype(BF16)
    field = dot(part, ru3[...], NN)
    centre = field[:, :nlon]
    image = (
        balance[0] * centre[:nlat]
        + balance[1] * pltpu.roll(field, wide - 1, 1)[:nlat, :nlon]
        + balance[2] * pltpu.roll(field, 1, 1)[:nlat, :nlon]
        + balance[3] * pltpu.roll(centre, tall - 1, 0)[:nlat]
        + balance[4] * pltpu.roll(centre, 1, 0)[:nlat]
    )
    misfit = weight * (image - inn)

    def longer(value):
        return jnp.concatenate([value, jnp.zeros((value.shape[0], wide - nlon), F32)], axis=1)

    def taller(value):
        return jnp.concatenate([value, jnp.zeros((tall - nlat, value.shape[1]), F32)], axis=0)

    across = (
        longer(balance[0] * misfit)
        + pltpu.roll(longer(balance[1] * misfit), 1, 1)
        + pltpu.roll(longer(balance[2] * misfit), wide - 1, 1)
    )
    along = pltpu.roll(taller(balance[3] * misfit), 1, 0) + pltpu.roll(taller(balance[4] * misfit), tall - 1, 0)
    grad = taller(across) + longer(along)
    back = dot(three(grad, 1), rub3[...], NT).T
    high, low = split(back)
    return dot(high, rl_hi[...], NN) + (dot(high, rl_lo[...], NN) + dot(low, rl_hi[...], NN))


def fine_kernel(bands, stripe, band_ref, *refs):
    wins, (inn, weight), consts = refs[:bands], refs[bands : bands + 2], refs[bands + 2 : bands + 8]
    outs, window = refs[bands + 8 : -1], refs[-1]
    turn, level = pl.program_id(0), pl.program_id(1)
    width = outs[0].shape[1]
    for s in range(bands):

        @pl.when(turn == s)
        def _():
            value = wins[s][level]
            window[:width, :] = value if value.shape[0] == width else unpacked(stripe, value, False)

    if width < window.shape[0]:
        window[width:, :] = jnp.zeros((window.shape[0] - width, window.shape[1]), F32)
    result = fine_level(window[...], inn[0], weight[0], *consts)
    for s in range(bands):

        @pl.when(turn == s)
        def _():
            outs[s][level] = result[:width]


def add_kernel(bands, band_ref, ctrl, *refs):
    pieces, out = refs[:bands], refs[-1]
    band = band_ref[0]
    for s in range(bands):
        owner = lax.rem(band - s + bands, bands)
        out[0, owner, 0] = ctrl[0, owner, 0] + pieces[s][0, 0]


def scalar_grid(grid, in_specs, out_specs, scratch=()):
    return pltpu.PrefetchScalarGridSpec(
        num_scalar_prefetch=1, grid=grid, in_specs=in_specs, out_specs=out_specs, scratch_shapes=scratch
    )


def whole_block(array):
    return pl.BlockSpec(array.shape, lambda *ids: (0,) * len(array.shape))


def chunks_of(owned):
    count = math.gcd(owned, 4)
    return [(owned // count * i, owned // count) for i in range(count)]


def body(controls, members, loc_lon, loc_lat, balance, innovation, obs_weight):
    bands, mates = lax.axis_size("band"), lax.axis_size("member")
    band = lax.axis_index("band")
    band_array = jnp.reshape(band, (1,)).astype(jnp.int32)
    held, levels, cy, nx = controls.shape
    ny = loc_lat.shape[0]
    cx = nx // mates
    owned = levels // bands
    width, deep = round_up(cx + 4, 8), round_up(cx + 4, 16)
    lanes = min(round_up(cy + 4, 128), ny)
    nlat, nlon = innovation.shape[1:]
    tall, wide = nlat + 8, round_up(nlon + 2, 128)
    scale = 1.0 / math.sqrt(held * mates - 1)

    turned = jnp.roll(loc_lat, (-cy * band, -cy * band), (0, 1))
    lat3, lat_t3 = outer_three(turned, 1), outer_three(turned.T, 1)
    lon3, lon_b3 = outer_three(loc_lon, 1), outer_three(loc_lon, 0)
    ru = jnp.asarray(edged_matrix(cx, wide, deep).T)
    ru3, rub3 = outer_three(ru, 0), outer_three(ru, 1)
    row = lax.broadcasted_iota(jnp.int32, (tall, lanes), 0)
    col = lax.broadcasted_iota(jnp.int32, (tall, lanes), 1)
    first, last = band == 0, band == bands - 1
    off = (first & ((row == tall - 1) | (col < 2))) | (last & ((row == nlat) | (col >= cy + 2)))
    rl = jnp.where(off, 0.0, jnp.asarray(edged_matrix(cy, tall, lanes)))
    rl3, (rl_hi, rl_lo) = outer_three(rl, 1), outer_split(rl)

    plan = chunks_of(owned)
    count = plan[0][1]
    ctrl_view = controls.reshape(held, bands, owned, cy, nx)
    mem_view = members.reshape(held, bands, owned, cy, nx)
    wrap_scratch = pltpu.VMEM((nx + 16, ny), F32)

    def shifted(value, s):
        if s % bands == 0:
            return value
        return lax.ppermute(value, "band", [(i, (i + s) % bands) for i in range(bands)])

    def sent(views, first_level, s):
        at = lax.rem(band - s + bands, bands)
        size, start = (held, 1, count, cy, nx), (0, at, first_level, 0, 0)
        return jnp.stack([lax.dynamic_slice(v, start, size)[:, 0] for v in views])

    def received(views, first_level):
        return [shifted(sent(views, first_level, s), -s) for s in range(1, bands)]

    def own_spec(first_level):
        return pl.BlockSpec((held, None, None, cy, nx), lambda l, b: (0, b[0], first_level + l, 0, 0))

    def piece_spec(at):
        return pl.BlockSpec((None, held, None, cy, nx), lambda l, b: (at, 0, l, 0, 0))

    def swapped_spec(parts, copies):
        return pl.BlockSpec((copies, parts, None, width, ny), lambda l, b: (0, 0, l, 0, 0))

    def operands(view, first_level, pieces):
        specs = [own_spec(first_level)] + [piece_spec(p[1]) for p in pieces]
        return [view] + [p[0] for p in pieces], specs

    field_spec = pl.BlockSpec((held, None, ny, nx), lambda l, b: (0, l, 0, 0))

    def fields(first_level, pieces):
        arrays, specs = operands(ctrl_view, first_level, pieces)

        def kernel(band_ref, *refs):
            for k in range(held):
                refs[-1][k] = field_of(refs[:bands], *refs[bands : bands + 2], k)

        return pl.pallas_call(
            kernel,
            grid_spec=scalar_grid((count,), specs + [whole_block(lat3), whole_block(lon3)], field_spec),
            out_shape=jax.ShapeDtypeStruct((held, count, ny, nx), F32),
            name="fields",
        )(band_array, *arrays, lat3, lon3)

    def stage_in(first_level, pieces, ready, coarse, single):
        arrays, specs = [], []
        if pieces is not None:
            arrays, specs = operands(mem_view, first_level, pieces[1])
            if ready is not None:
                arrays, specs = arrays + [ready], specs + [field_spec]
            else:
                more, more_specs = operands(ctrl_view, first_level, pieces[0])
                arrays += more + [lat3, lon3]
                specs += more_specs + [whole_block(lat3), whole_block(lon3)]
        if coarse is not None:
            last = coarse[0].shape[0] - 1
            arrays += coarse
            specs += [pl.BlockSpec((None, None, coarse[0].shape[2], lanes), lambda l, b: (last, l, 0, 0))] * bands
        parts = (pieces is not None) + (coarse is not None)
        copies = 1 if single else mates

        def kernel(band_ref, *refs):
            refs = list(refs)
            wrapped, out = refs.pop(), refs.pop()
            if pieces is not None:
                if ready is not None:
                    field = lambda k: refs[bands][k]
                else:
                    field = functools.partial(field_of, refs[bands : 2 * bands], *refs[2 * bands : 2 * bands + 2])
                increment_of(scale, field, refs[:bands], wrapped, out)
            if coarse is not None:
                overlapped(cy, refs[-bands:], out)

        return pl.pallas_call(
            kernel,
            grid_spec=scalar_grid((count,), specs, swapped_spec(parts, copies), [wrap_scratch]),
            out_shape=jax.ShapeDtypeStruct((copies, parts, count, width, ny), F32),
            name="stage_in",
        )(band_array, *arrays)

    def stage_out(swapped, fine_out):
        arrays, specs = [swapped], [swapped_spec(swapped.shape[1], mates)]
        joined = fine_out is not None
        tight = joined and 2 * cy == lanes
        parts, high = (1, width + 8) if tight else (1 + joined, width)
        if joined:
            arrays += fine_out
            specs += [pl.BlockSpec((None, None, width, lanes), lambda l, b: (0, l, 0, 0))] * bands

        def kernel(band_ref, *refs):
            outs = refs[len(arrays) :]
            for s, window in enumerate(windows_of(cy, refs[0])):
                window = window[:, :lanes]
                result = refs[1 + (bands - s) % bands][...] if joined else None
                if tight:
                    outs[s][0] = packed(cy, window, result)
                else:
                    outs[s][0] = window
                    if joined:
                        outs[s][1] = result

        return pl.pallas_call(
            kernel,
            grid_spec=scalar_grid(
                (count,), specs, [pl.BlockSpec((parts, None, high, lanes), lambda l, b: (0, l, 0, 0))] * bands
            ),
            out_shape=[jax.ShapeDtypeStruct((parts, count, high, lanes), F32)] * bands,
            name="stage_out",
        )(band_array, *arrays)

    def adjoint(swapped, first_level, perts):
        arrays = [swapped, mem_view] + [p[0] for p in perts] + [lat_t3, lon_b3]
        specs = [swapped_spec(swapped.shape[1], mates), own_spec(first_level)] + [piece_spec(p[1]) for p in perts]
        specs += [whole_block(lat_t3), whole_block(lon_b3)]

        def kernel(band_ref, swap_ref, *refs):
            adjoint_of(scale, swap_ref, refs[:bands], *refs[bands : bands + 2], refs[-1], refs[bands + 2 : -1])

        return pl.pallas_call(
            kernel,
            grid_spec=scalar_grid(
                (count,),
                specs,
                [pl.BlockSpec((held, None, cy, nx), lambda l, b: (0, l, 0, 0))] * bands,
                [wrap_scratch],
            ),
            out_shape=[jax.ShapeDtypeStruct((held, count, cy, nx), F32)] * bands,
            name="adjoint",
        )(band_array, *arrays)

    def fine(wins, first_level):
        def level(o, l, b):
            return (lax.rem(b[0] - o + bands, bands) * owned + first_level + l, 0, 0)

        consts = (balance, rl3, ru3, rl_hi, rl_lo, rub3)
        return pl.pallas_call(
            functools.partial(fine_kernel, bands, cy),
            grid_spec=scalar_grid(
                (bands, count),
                [pl.BlockSpec((None, count, wins[0].shape[2], lanes), lambda o, l, b: (0, 0, 0, 0))] * bands
                + [pl.BlockSpec((1, nlat, nlon), level)] * 2
                + [whole_block(c) for c in consts],
                [pl.BlockSpec((None, count, width, lanes), lambda o, l, b: (0, 0, 0, 0))] * bands,
                [pltpu.VMEM((deep, lanes), F32)],
            ),
            out_shape=[jax.ShapeDtypeStruct((1, count, width, lanes), F32)] * bands,
            name="fine",
        )(band_array, *wins, innovation, obs_weight, *consts)

    def added(result, pieces, first_level):
        block = pl.BlockSpec((1, bands, 1, cy, nx), lambda k, l, b: (k, 0, first_level + l, 0, 0))
        piece = pl.BlockSpec((1, 1, cy, nx), lambda k, l, b: (k, l, 0, 0))
        carried = [] if result is None else [result]
        return pl.pallas_call(
            functools.partial(add_kernel, bands),
            grid_spec=scalar_grid(
                (held, count),
                [block] + [piece] * bands + [pl.BlockSpec(memory_space=pl.ANY)] * len(carried),
                block,
            ),
            out_shape=jax.ShapeDtypeStruct(ctrl_view.shape, F32),
            input_output_aliases={2 + bands: 0} if carried else {},
            name="added",
        )(band_array, ctrl_view, *pieces, *carried)

    swap = functools.partial(lax.all_to_all, split_axis=0, concat_axis=0, tiled=True)
    total = len(plan)
    pieces, small, result = [], None, None
    for i, (first, _) in enumerate(plan):
        if i in (0, total - 1):
            sides = []
            for view in (ctrl_view, mem_view):
                sides.append([(p, 0) for p in received((view,), first)])
        else:
            pair = received((ctrl_view, mem_view), first)
            sides = [[(p, 0) for p in pair], [(p, 1) for p in pair]]
        pieces.append(sides)
    for t in range(total + 2):
        now, middle, old = (i if 0 <= i < total else None for i in (t, t - 1, t - 2))
        level = None if now is None else plan[now][0]
        ready = None
        if now == total - 1:
            ready = fields(level, pieces[now][0])
        coarse = None if old is None else [small[(bands - s) % bands] for s in range(bands)]
        value = None
        if now is not None or old is not None:
            value = stage_in(level, None if now is None else pieces[now], ready, coarse, t == total + 1)
        if value is not None:
            if t == total + 1:
                value = lax.all_gather(value, "member", axis=0, tiled=True)
            else:
                value = swap(value, "member")
        fine_out = None
        if middle is not None:
            fine_out = fine(small, plan[middle][0])
        sending = None
        if now is not None:
            sending = stage_out(value, fine_out)
        elif fine_out is not None:
            sending = [fine_out[(bands - s) % bands] for s in range(bands)]
        if sending is not None:
            small = [shifted(p, s) for s, p in enumerate(sending)]
        if old is not None:
            back = adjoint(value, plan[old][0], pieces[old][1])
            back = [shifted(p, s) for s, p in enumerate(back)]
            result = added(result, back, plan[old][0])
    return result.reshape(controls.shape)


def solution(mesh):
    return jax.shard_map(
        body,
        mesh=mesh,
        in_specs=(
            P("member", None, "band", None),
            P("member", None, "band", None),
            P(),
            P(),
            P(None, "band", "member"),
            P(None, "band", "member"),
            P(None, "band", "member"),
        ),
        out_specs=P("member", None, "band", None),
        check_vma=False,
    )
```
